32 devices in a mesh: language: 2 (over core), fsdp: 16 (over z, y, x).
Axes of the slice: x: 2, y: 2, z: 4, core: 2. Of those that a mesh axis runs over, the one named last changes fastest.
Arguments:
- hidden: bfloat16 [4, 2048, 5120], P('language', 'fsdp'), may hold values from -60 to 60
- latent_grad: bfloat16 [4, 2048, 64], P('language', 'fsdp'), may hold values from -0.3125 to 0.3125
- lang_ids: int32 [4], P('language'), may hold values from 0 to 3, each once
- old_weights: float32 [4], replicated, may hold values from 0.02 to 0.2
- param: float32 [5120, 64], P('fsdp'), may hold values from -6 to 6
- first_moment: float32 [5120, 64], P('fsdp'), may hold values from -6 to 6
- second_moment: float32 [5120, 64], P('fsdp'), may hold values from 0.25 to 4
Outputs:
- new_param: float32 [5120, 64], P('fsdp')
- new_first: float32 [5120, 64], P('fsdp')
- new_second: float32 [5120, 64], P('fsdp')
- new_logweights: float32 [4], replicated
The draws below stay inside these ranges and needn't reach their ends.
Inputs may be any that keep to these rules, and one draw needn't show every extreme that they name: `lang_ids`: each id appears in exactly one slot.
All inputs are finite; a program needn't handle non-finite values.
Results may differ from the reference program's by a relative error of at most 0.0003.
Values may be sent and summed in bfloat16 or wider, within the bound.
No kernel may reach another device: no remote copies, remote signals or barrier semaphores. Data moves between devices by JAX's collectives and lax.ppermute only.
A program may use at most 64 MiB of HBM per device.

```python
import math
import jax
import jax.numpy as jnp
from jax import lax

D = 5120
RANK = 32
STEP = 100
LANGS = 4
TOKENS = 2048


def draw_hidden(key, part):
    key_lang, key_feat, key_base = jax.random.split(key, 3)
    lang_scale = jnp.exp(jax.random.uniform(key_lang, (LANGS, 1, 1), minval=math.log(0.5), maxval=math.log(2.0)))
    position = jnp.arange(D, dtype=jnp.float32) / D
    feat_scale = jnp.exp(0.55 * position + 0.3 * jax.random.normal(key_feat, (D,), dtype=jnp.float32))
    base = jax.random.normal(key_base, (LANGS, TOKENS, D), dtype=jnp.float32)
    values = jnp.clip(base * lang_scale * feat_scale[None, None, :], -60.0, 60.0)
    return values.astype(jnp.bfloat16)


def block_levels(own_key, dims, shards, smallest, top_value):
    def one(axis_at, parts):
        heights = jax.random.uniform(jax.random.fold_in(jax.random.fold_in(own_key, 6), axis_at), (parts,), jnp.float32, smallest / len(shards), top_value / len(shards))
        return jnp.repeat(jnp.exp(heights), dims[axis_at] // parts).reshape((-1,) + (1,) * (len(dims) - axis_at - 1))

    loudness = one(*shards[0])
    for cut in shards[1:]:
        loudness = loudness * one(*cut)
    return loudness


def normal_values(key, shape, deviation, most, shards=(), kind=jnp.bfloat16):
    array = jax.random.normal(key, shape, jnp.float32) * deviation
    if len(shards) > 0:
        array = block_levels(key, shape, shards, -0.22, 0.18) * array
    return jnp.clip(array, min=-most, max=most).astype(kind)


def setup_inputs(seed: int = 0) -> dict:
    streams_of = jax.random.split(jax.random.key(seed), 8)
    hidden = draw_hidden(jax.random.fold_in(streams_of[7], 71), 0)
    latent_grad = normal_values(streams_of[1], (LANGS, TOKENS, 2 * RANK), (1.0 / TOKENS ** 0.5), 0.3125, ((0, 2), (1, 16)))
    lang_ids = jax.random.permutation(streams_of[2], LANGS).astype(jnp.int32)
    old_weights = jnp.clip(jnp.exp(jax.random.uniform(streams_of[3], (LANGS,), jnp.float32, math.log(0.02), math.log(0.2))), 0.02, 0.2)
    param = normal_values(streams_of[4], (D, 2 * RANK), 1.0, 6.0, ((0, 16),), jnp.float32)
    first_moment = normal_values(streams_of[5], (D, 2 * RANK), 1.0, 6.0, ((0, 16),), jnp.float32)
    second_moment = jnp.clip(jnp.exp(math.log(4.0) - 2.7725887 * jax.random.uniform(streams_of[6], (D, 2 * RANK), jnp.float32) ** block_levels(streams_of[6], (D, 2 * RANK), ((0, 16),), -0.2, 0.2)), 0.25, 4.0)
    return {"hidden": hidden, "latent_grad": latent_grad, "lang_ids": lang_ids, "old_weights": old_weights, "param": param, "first_moment": first_moment, "second_moment": second_moment}


def slot_gradient(pair):
    feats, latents = pair
    return jnp.einsum('td,tr->dr', feats.astype(jnp.float32), latents.astype(jnp.float32), precision=lax.Precision.HIGHEST)

def reference(hidden, latent_grad, lang_ids, old_weights, param, first_moment, second_moment):
    slot_grad = lax.map(slot_gradient, (hidden, latent_grad))
    total = lax.optimization_barrier(jnp.sum(slot_grad, axis=0))
    dots = jnp.einsum('ldr,dr->l', slot_grad, total, precision=lax.Precision.HIGHEST)
    square = jnp.sum(total * total) + 1e-06
    onehot = (lang_ids[:, None] == jnp.arange(LANGS, dtype=jnp.int32)[None, :]).astype(jnp.float32)
    align = jnp.dot(dots, onehot, precision=lax.Precision.HIGHEST) / square
    logits = jnp.log(old_weights) + LANGS * align
    new_logweights = logits - jnp.log(jnp.sum(jnp.exp(logits)))
    weights = jnp.exp(new_logweights)
    slot_weight = jnp.dot(onehot, weights, precision=lax.Precision.HIGHEST)
    update = jnp.einsum('l,ldr->dr', slot_weight, slot_grad, precision=lax.Precision.HIGHEST)
    new_first = 0.9 * first_moment + 0.1 * update
    new_second = 0.95 * second_moment + 0.05 * update * update
    first_hat = new_first / (1.0 - 0.9 ** STEP)
    second_hat = new_second / (1.0 - 0.95 ** STEP)
    new_param = param - 0.02 * (first_hat / (jnp.sqrt(second_hat) + 1e-08) + 0.1 * param)
    return (new_param, new_first, new_second, new_logweights)
```

```python
import functools
import math

import jax
import jax.numpy as jnp
from jax import lax
from jax.experimental import pallas as pl
from jax.experimental.pallas import tpu as pltpu
from jax.sharding import PartitionSpec as P

STEP = 100
SUB = 8
LANES = 128
FINE = 32.0
TOP = 32766.0
VMEM_LIMIT = 24 * 1024 * 1024
BOTH = ("language", "fsdp")


def whole(memory=pltpu.VMEM):
    return pl.BlockSpec(memory_space=memory)


def params():
    return pltpu.CompilerParams(vmem_limit_bytes=VMEM_LIMIT)


def encode(block):
    rows, lanes = block.shape
    half = rows // 2
    top = jnp.max(jnp.abs(block).reshape(rows // SUB, SUB, lanes), axis=0)
    step = jnp.ceil(jnp.log2(jnp.maximum(top, 1e-30)) * FINE)
    scale = jnp.exp2(step * (-1.0 / FINE)) * TOP
    codes = block.reshape(rows // SUB, SUB, lanes) * scale[None] + 32768.5
    codes = codes.astype(jnp.int32).reshape(rows, lanes)
    words = lax.shift_left(codes[:half], 16) | codes[half:]
    return words, step.astype(jnp.int32)


def decode(words, step):
    half, lanes = words.shape
    scale = jnp.exp2(step.astype(jnp.float32) * (1.0 / FINE)) * (1.0 / TOP)
    high = lax.shift_right_logical(words, 16).astype(jnp.float32) - 32768.0
    low = (words & 65535).astype(jnp.float32) - 32768.0
    both = jnp.concatenate([high, low], axis=0).reshape(2 * half // SUB, SUB, lanes)
    return (both * scale[None]).reshape(2 * half, lanes)


def spot(me, parity, index, bits):
    p = jnp.bitwise_xor(me, index)
    swap = (p ^ (p >> 1)) & 1 & parity
    p = p ^ (swap | (swap << 1))
    out = jnp.int32(0)
    for k in range(bits):
        out = out | (((p >> k) & 1) << (bits - 1 - k))
    return out


def first_kernel(blocks, rows, where_ref, hidden_ref, latent_ref, keep_ref, send_ref):
    bits = blocks.bit_length() - 1
    slots, tokens, width = hidden_ref.shape
    rank = latent_ref.shape[1]
    zero = jnp.zeros((rank, tokens), latent_ref.dtype)
    left = jnp.concatenate(
        [jnp.concatenate([latent_ref[a] if a == b else zero for b in range(slots)], axis=1) for a in range(slots)], axis=0
    )
    grad = jnp.dot(left, hidden_ref[...].reshape(slots * tokens, width), preferred_element_type=jnp.float32).T
    per = width // rows
    for k in range(per):
        at = spot(where_ref[0], where_ref[1], pl.program_id(0) * per + k, bits)
        block = grad[k * rows : (k + 1) * rows]

        @pl.when(at < blocks // 2)
        def _():
            keep_ref[at] = block

        @pl.when(at >= blocks // 2)
        def _():
            words, step = encode(block)
            send_ref[at - blocks // 2, : rows // 2] = words
            send_ref[at - blocks // 2, rows // 2 :] = step


def first(hidden, latent, where, blocks):
    slots, tokens, dim = hidden.shape
    rows = dim // blocks
    width = math.lcm(rows, LANES)
    lanes = slots * latent.shape[1]
    return pl.pallas_call(
        functools.partial(first_kernel, blocks, rows),
        grid_spec=pltpu.PrefetchScalarGridSpec(
            num_scalar_prefetch=1,
            grid=(dim // width,),
            in_specs=[
                pl.BlockSpec((slots, tokens, width), lambda q, w: (0, 0, q)),
                pl.BlockSpec(latent.shape, lambda q, w: (0, 0, 0)),
            ],
            out_specs=[
                pl.BlockSpec((blocks // 2, rows, lanes), lambda q, w: (0, 0, 0)),
                pl.BlockSpec((blocks // 2, rows // 2 + SUB, lanes), lambda q, w: (0, 0, 0)),
            ],
        ),
        out_shape=[
            jax.ShapeDtypeStruct((blocks // 2, rows, lanes), jnp.float32),
            jax.ShapeDtypeStruct((blocks // 2, rows // 2 + SUB, lanes), jnp.int32),
        ],
        compiler_params=params(),
    )(where, hidden, latent)


def added(got_ref, keep_ref, at):
    half = got_ref.shape[1] - SUB
    return keep_ref[at] + decode(got_ref[at, :half], got_ref[at, half:])


def middle_kernel(got_ref, keep_ref, left_ref, send_ref):
    blocks = keep_ref.shape[0]
    half = keep_ref.shape[1] // 2
    for k in range(blocks // 2):
        words, step = encode(added(got_ref, keep_ref, blocks // 2 + k))
        send_ref[k, :half] = words
        send_ref[k, half:] = step
    for k in range(blocks // 2):
        left_ref[k] = added(got_ref, keep_ref, k)


def middle(got, keep):
    blocks, rows, lanes = keep.shape
    return pl.pallas_call(
        middle_kernel,
        in_specs=[whole(), whole()],
        out_specs=[whole(), whole()],
        out_shape=[
            jax.ShapeDtypeStruct((blocks // 2, rows, lanes), jnp.float32),
            jax.ShapeDtypeStruct((blocks // 2, rows // 2 + SUB, lanes), jnp.int32),
        ],
        compiler_params=params(),
    )(got, keep)


def last_kernel(ids_ref, got_ref, keep_ref, out_ref):
    rows, lanes = keep_ref.shape[1:]
    slots = ids_ref.shape[0]
    out_ref[:rows] = added(got_ref, keep_ref, 0)
    slot = lax.broadcasted_iota(jnp.int32, (SUB, lanes), 1) // (lanes // slots)
    row = jnp.zeros((SUB, lanes), jnp.float32)
    for s in range(slots):
        row = jnp.where(slot == s, ids_ref[s].astype(jnp.float32), row)
    out_ref[rows:] = row


def last(ids, got, keep):
    _, rows, lanes = keep.shape
    return pl.pallas_call(
        last_kernel,
        in_specs=[whole(pltpu.SMEM), whole(), whole()],
        out_specs=whole(),
        out_shape=jax.ShapeDtypeStruct((rows + SUB, lanes), jnp.float32),
        compiler_params=params(),
    )(ids, got, keep)


def spread(x, rank):
    lanes = x.shape[1]
    out = x
    shift = rank
    while shift < lanes:
        out = out + pltpu.roll(out, shift, 1)
        shift *= 2
    return out


def dots_kernel(rank, every_ref, out_ref):
    groups, rows, lanes = every_ref.shape
    rows -= SUB
    total = every_ref[0, :rows]
    for g in range(1, groups):
        total = total + every_ref[g, :rows]
    total = spread(total, rank)
    out_ref[...] = jnp.zeros_like(out_ref)
    for g in range(groups):
        out_ref[g : g + 1] = jnp.sum(every_ref[g, :rows] * total, axis=0, keepdims=True)
    out_ref[groups : groups + 1] = jnp.sum(total * total, axis=0, keepdims=True)


def dots(every, rank):
    groups, _, lanes = every.shape
    return pl.pallas_call(
        functools.partial(dots_kernel, rank),
        in_specs=[whole()],
        out_specs=whole(),
        out_shape=jax.ShapeDtypeStruct((pl.cdiv(groups + 1, SUB) * SUB, lanes), jnp.float32),
        compiler_params=params(),
    )(every)


def turn_kernel(every_ref, out_ref):
    groups, rows, _ = every_ref.shape
    for g in range(groups):
        out_ref[g] = every_ref[g, : rows - SUB].T


def turn(every):
    groups, rows, lanes = every.shape
    return pl.pallas_call(
        turn_kernel,
        in_specs=[whole()],
        out_specs=whole(),
        out_shape=jax.ShapeDtypeStruct((groups, lanes, rows - SUB), jnp.float32),
        compiler_params=params(),
    )(every)


def final_kernel(
    sums_ref, every_ref, grad_ref, old_ref, param_ref, first_ref, second_ref, new_param_ref, new_first_ref, new_second_ref, log_ref
):
    groups, lanes, _ = grad_ref.shape
    langs = old_ref.shape[1]
    rank = param_ref.shape[0]
    slots = lanes // rank
    parts = sums_ref[:groups]
    square = jnp.sum(sums_ref[groups : groups + 1, :rank], axis=1, keepdims=True) + 1e-06
    ids = jnp.concatenate([every_ref[g, :1] for g in range(groups)], axis=0)
    at = lax.broadcasted_iota(jnp.int32, (1, langs), 1)
    align = jnp.zeros((1, langs), jnp.float32)
    for k in range(langs):
        one = jnp.sum(jnp.where(ids == float(k), parts, 0.0), axis=1, keepdims=True)
        align = jnp.where(at == k, jnp.sum(one, axis=0, keepdims=True), align)
    logits = jnp.log(old_ref[...]) + float(langs) * (align / square)
    logs = logits - jnp.log(jnp.sum(jnp.exp(logits), axis=1, keepdims=True))
    log_ref[...] = logs
    weights = jnp.exp(logs)
    update = None
    for g in range(groups):
        for s in range(slots):
            own = ids[g : g + 1, s * rank : s * rank + 1]
            weight = jnp.zeros((1, 1), jnp.float32)
            for k in range(langs):
                weight = weight + jnp.where(own == float(k), weights[:, k : k + 1], 0.0)
            term = weight * grad_ref[g, s * rank : (s + 1) * rank]
            update = term if update is None else update + term
    new_first = 0.9 * first_ref[...] + 0.1 * update
    new_second = 0.95 * second_ref[...] + 0.05 * update * update
    first_hat = new_first / (1.0 - 0.9**STEP)
    second_hat = new_second / (1.0 - 0.95**STEP)
    param = param_ref[...]
    new_param_ref[...] = param - 0.02 * (first_hat / (jnp.sqrt(second_hat) + 1e-08) + 0.1 * param)
    new_first_ref[...] = new_first
    new_second_ref[...] = new_second


def final(sums, every, grads, old, param, first_moment, second_moment):
    groups, rows, lanes = every.shape
    shape = jax.ShapeDtypeStruct(param.shape, jnp.float32)
    whole_of = lambda x: pl.BlockSpec(x.shape, lambda i: (0,) * len(x.shape))
    return pl.pallas_call(
        final_kernel,
        grid=(1,),
        in_specs=[
            whole_of(sums),
            pl.BlockSpec((groups, SUB, lanes), lambda i: (0, rows // SUB - 1, 0)),
            whole_of(grads),
            whole_of(old),
            whole_of(param),
            whole_of(param),
            whole_of(param),
        ],
        out_specs=[whole_of(param), whole_of(param), whole_of(param), whole_of(old)],
        out_shape=[shape, shape, shape, jax.ShapeDtypeStruct(old.shape, jnp.float32)],
        compiler_params=params(),
    )(sums, every, grads, old, param, first_moment, second_moment)


def local(groups, blocks, hidden, latent_grad, lang_ids, old_weights, param, first_moment, second_moment):
    bits = blocks.bit_length() - 1
    rank = latent_grad.shape[2]

    def flip(even, odd):
        pairs = [(g * blocks + f, g * blocks + (f ^ (1 << (odd if g % 2 else even)))) for g in range(groups) for f in range(blocks)]
        return functools.partial(lax.ppermute, axis_name=BOTH, perm=pairs)

    where = jnp.stack([lax.axis_index("fsdp"), lax.axis_index("language") % 2]).astype(jnp.int32)
    keep, send = first(hidden, latent_grad.transpose(0, 2, 1), where, blocks)
    for k in range(bits):
        got = flip(k, 1 - k if k < 2 else k)(send)
        if k < bits - 1:
            keep, send = middle(got, keep)
    mine = last(lang_ids, got, keep)
    every = lax.all_gather(mine, "language")
    sums = dots(every, rank)
    grads = turn(every)
    for k in range(bits):
        sums = sums + flip(k, k)(sums)
    new_param, new_first, new_second, logs = final(
        sums, every, grads, old_weights[None], param.T, first_moment.T, second_moment.T
    )
    return new_param.T, new_first.T, new_second.T, logs[0]


def solution(mesh):
    placed = (
        P("language", "fsdp", None),
        P("language", "fsdp", None),
        P("language"),
        P(),
        P("fsdp", None),
        P("fsdp", None),
        P("fsdp", None),
    )
    return jax.shard_map(
        functools.partial(local, mesh.shape["language"], mesh.shape["fsdp"]),
        mesh=mesh,
        in_specs=placed,
        out_specs=(P("fsdp", None), P("fsdp", None), P("fsdp", None), P()),
        check_vma=False,
    )
```

```python
import functools
import math

import jax
import jax.numpy as jnp
from jax import lax
from jax.experimental import pallas as pl
from jax.experimental.pallas import tpu as pltpu
from jax.sharding import PartitionSpec as P

STEP = 100
SUB = 8
LANES = 128
FINE = 32.0
TOP = 32766.0
VMEM_LIMIT = 24 * 1024 * 1024
BOTH = ("language", "fsdp")


def whole(memory=pltpu.VMEM):
    return pl.BlockSpec(memory_space=memory)


def params():
    return pltpu.CompilerParams(vmem_limit_bytes=VMEM_LIMIT)


def encode(block):
    rows, lanes = block.shape
    half = rows // 2
    top = jnp.max(jnp.abs(block).reshape(rows // SUB, SUB, lanes), axis=0)
    step = jnp.ceil(jnp.log2(jnp.maximum(top, 1e-30)) * FINE)
    scale = jnp.exp2(step * (-1.0 / FINE)) * TOP
    codes = block.reshape(rows // SUB, SUB, lanes) * scale[None] + 32768.5
    codes = codes.astype(jnp.int32).reshape(rows, lanes)
    words = lax.shift_left(codes[:half], 16) | codes[half:]
    return words, step.astype(jnp.int32)


def decode(words, step):
    half, lanes = words.shape
    scale = jnp.exp2(step.astype(jnp.float32) * (1.0 / FINE)) * (1.0 / TOP)
    high = lax.shift_right_logical(words, 16).astype(jnp.float32) - 32768.0
    low = (words & 65535).astype(jnp.float32) - 32768.0
    both = jnp.concatenate([high, low], axis=0).reshape(2 * half // SUB, SUB, lanes)
    return (both * scale[None]).reshape(2 * half, lanes)


def place(blocks, parity, chain, half, index):
    bits = blocks.bit_length() - 1
    p = (half << parity) | (chain << (bits - 1))
    for k in range(1, bits - 1):
        bit = (index >> (bits - 2 - k)) & 1
        p |= bit << (1 - parity if k == 1 else k)
    return p


def grad_kernel(blocks, parts, coded, hidden_ref, latent_ref, *refs):
    out_refs, (hidden, latent, turned, sems) = refs[: len(parts)], refs[len(parts) :]
    count, slots, tokens, width = hidden.shape
    rank = latent.shape[1]
    rows = hidden_ref.shape[2] // blocks
    per = blocks // 4
    me, parity = lax.axis_index("fsdp"), lax.axis_index("language") % 2
    starts = []
    for chain, half in parts:
        for k in range(per):
            even, odd = place(blocks, 0, chain, half, k), place(blocks, 1, chain, half, k)
            starts.append(jnp.bitwise_xor(me, jnp.where(parity == 1, odd, even)) * rows)
    small = pltpu.make_async_copy(latent_ref, latent, sems.at[count])
    small.start()
    copies, bases = [], []
    for k in range(count):
        base = jnp.minimum(starts[k] // LANES, (hidden_ref.shape[2] - width) // LANES) * LANES
        bases.append(pl.multiple_of(base, LANES))
        base = bases[k]
        copies.append(pltpu.make_async_copy(hidden_ref.at[:, :, pl.ds(base, width)], hidden.at[k], sems.at[k]))
        copies[k].start()
    small.wait()
    zero = jnp.zeros((rank, tokens), latent.dtype)
    left = jnp.concatenate(
        [jnp.concatenate([latent[a] if a == b else zero for b in range(slots)], axis=1) for a in range(slots)], axis=0
    )
    for k in range(count):
        copies[k].wait()
        grad = jnp.dot(left, hidden[k].reshape(slots * tokens, width), preferred_element_type=jnp.float32)
        turned[k % 2] = grad.T
        block = turned[k % 2, pl.ds(pl.multiple_of(starts[k] - bases[k], SUB), rows)]
        out_ref = out_refs[k // per]
        if coded:
            out_ref[k % per, : rows // 2], out_ref[k % per, rows // 2 :] = encode(block)
        else:
            out_ref[k % per] = block


def slot_grads(hidden, latent, blocks, parts, coded):
    slots, tokens, dim = hidden.shape
    rows = dim // blocks
    lanes = slots * latent.shape[1]
    reach = max(rows * k % LANES for k in range(blocks)) + rows
    width = pl.cdiv(reach, LANES) * LANES
    count = len(parts) * blocks // 4
    shape = (
        jax.ShapeDtypeStruct((blocks // 4, rows // 2 + SUB, lanes), jnp.int32)
        if coded
        else jax.ShapeDtypeStruct((blocks // 4, rows, lanes), jnp.float32)
    )
    return pl.pallas_call(
        functools.partial(grad_kernel, blocks, parts, coded),
        in_specs=[whole(pltpu.HBM), whole(pltpu.HBM)],
        out_specs=[whole()] * len(parts),
        out_shape=[shape] * len(parts),
        scratch_shapes=[
            pltpu.VMEM((count, slots, tokens, width), hidden.dtype),
            pltpu.VMEM(latent.shape, latent.dtype),
            pltpu.VMEM((2, width, lanes), jnp.float32),
            pltpu.SemaphoreType.DMA((count + 1,)),
        ],
        compiler_params=params(),
    )(hidden, latent)


def added(got_ref, keep_ref, at):
    half = got_ref.shape[1] - SUB
    return keep_ref[at] + decode(got_ref[at, :half], got_ref[at, half:])


def middle_kernel(got_ref, keep_ref, left_ref, send_ref):
    blocks = keep_ref.shape[0]
    half = keep_ref.shape[1] // 2
    for k in range(blocks // 2):
        words, step = encode(added(got_ref, keep_ref, blocks // 2 + k))
        send_ref[k, :half] = words
        send_ref[k, half:] = step
    for k in range(blocks // 2):
        left_ref[k] = added(got_ref, keep_ref, k)


def middle(got, keep):
    blocks, rows, lanes = keep.shape
    return pl.pallas_call(
        middle_kernel,
        in_specs=[whole(), whole()],
        out_specs=[whole(), whole()],
        out_shape=[
            jax.ShapeDtypeStruct((blocks // 2, rows, lanes), jnp.float32),
            jax.ShapeDtypeStruct((blocks // 2, rows // 2 + SUB, lanes), jnp.int32),
        ],
        compiler_params=params(),
    )(got, keep)


def pass_kernel(got_ref, keep_ref, send_ref):
    half = keep_ref.shape[1] // 2
    send_ref[0, :half], send_ref[0, half:] = encode(added(got_ref, keep_ref, 0))


def passed(got, keep):
    return pl.pallas_call(
        pass_kernel,
        in_specs=[whole(), whole()],
        out_specs=whole(),
        out_shape=jax.ShapeDtypeStruct(got.shape, got.dtype),
        compiler_params=params(),
    )(got, keep)


def last_kernel(ids_ref, got_ref, keep_ref, across_ref, out_ref):
    rows, lanes = keep_ref.shape[1:]
    slots = ids_ref.shape[1]
    half = rows // 2
    out_ref[:rows] = added(got_ref, keep_ref, 0) + decode(across_ref[0, :half], across_ref[0, half:])
    slot = lax.broadcasted_iota(jnp.int32, (SUB, lanes), 1) // (lanes // slots)
    row = jnp.zeros((SUB, lanes), jnp.float32)
    for s in range(slots):
        row = jnp.where(slot == s, ids_ref[:, s : s + 1].astype(jnp.float32), row)
    out_ref[rows:] = row


def last(ids, got, keep, across):
    _, rows, lanes = keep.shape
    return pl.pallas_call(
        last_kernel,
        in_specs=[whole(), whole(), whole(), whole()],
        out_specs=whole(),
        out_shape=jax.ShapeDtypeStruct((rows + SUB, lanes), jnp.float32),
        compiler_params=params(),
    )(ids, got, keep, across)


def spread(x, rank):
    lanes = x.shape[1]
    out = x
    shift = rank
    while shift < lanes:
        out = out + pltpu.roll(out, shift, 1)
        shift *= 2
    return out


def dots_kernel(rank, every_ref, out_ref):
    groups, rows, lanes = every_ref.shape
    rows -= SUB
    total = every_ref[0, :rows]
    for g in range(1, groups):
        total = total + every_ref[g, :rows]
    total = spread(total, rank)
    out_ref[...] = jnp.zeros_like(out_ref)
    for g in range(groups):
        out_ref[g : g + 1] = jnp.sum(every_ref[g, :rows] * total, axis=0, keepdims=True)
    out_ref[groups : groups + 1] = jnp.sum(total * total, axis=0, keepdims=True)


def dots(every, rank):
    groups, _, lanes = every.shape
    return pl.pallas_call(
        functools.partial(dots_kernel, rank),
        in_specs=[whole()],
        out_specs=whole(),
        out_shape=jax.ShapeDtypeStruct((pl.cdiv(groups + 1, SUB) * SUB, lanes), jnp.float32),
        compiler_params=params(),
    )(every)


def turn_kernel(every_ref, out_ref):
    groups, rows, _ = every_ref.shape
    for g in range(groups):
        out_ref[g] = every_ref[g, : rows - SUB].T


def turn(every):
    groups, rows, lanes = every.shape
    return pl.pallas_call(
        turn_kernel,
        in_specs=[whole()],
        out_specs=whole(),
        out_shape=jax.ShapeDtypeStruct((groups, lanes, rows - SUB), jnp.float32),
        compiler_params=params(),
    )(every)


def final_kernel(
    sums_ref, every_ref, grad_ref, old_ref, param_ref, first_ref, second_ref, new_param_ref, new_first_ref, new_second_ref, log_ref
):
    groups, lanes, _ = grad_ref.shape
    langs = old_ref.shape[1]
    rank = param_ref.shape[0]
    slots = lanes // rank
    parts = sums_ref[:groups]
    square = jnp.sum(sums_ref[groups : groups + 1, :rank], axis=1, keepdims=True) + 1e-06
    ids = jnp.concatenate([every_ref[g, :1] for g in range(groups)], axis=0)
    at = lax.broadcasted_iota(jnp.int32, (1, langs), 1)
    align = jnp.zeros((1, langs), jnp.float32)
    for k in range(langs):
        one = jnp.sum(jnp.where(ids == float(k), parts, 0.0), axis=1, keepdims=True)
        align = jnp.where(at == k, jnp.sum(one, axis=0, keepdims=True), align)
    logits = jnp.log(old_ref[...]) + float(langs) * (align / square)
    logs = logits - jnp.log(jnp.sum(jnp.exp(logits), axis=1, keepdims=True))
    log_ref[...] = logs
    weights = jnp.exp(logs)
    update = None
    for g in range(groups):
        for s in range(slots):
            own = ids[g : g + 1, s * rank : s * rank + 1]
            weight = jnp.zeros((1, 1), jnp.float32)
            for k in range(langs):
                weight = weight + jnp.where(own == float(k), weights[:, k : k + 1], 0.0)
            term = weight * grad_ref[g, s * rank : (s + 1) * rank]
            update = term if update is None else update + term
    new_first = 0.9 * first_ref[...] + 0.1 * update
    new_second = 0.95 * second_ref[...] + 0.05 * update * update
    first_hat = new_first / (1.0 - 0.9**STEP)
    second_hat = new_second / (1.0 - 0.95**STEP)
    param = param_ref[...]
    new_param_ref[...] = param - 0.02 * (first_hat / (jnp.sqrt(second_hat) + 1e-08) + 0.1 * param)
    new_first_ref[...] = new_first
    new_second_ref[...] = new_second


def final(sums, every, grads, old, param, first_moment, second_moment):
    groups, rows, lanes = every.shape
    shape = jax.ShapeDtypeStruct(param.shape, jnp.float32)
    whole_of = lambda x: pl.BlockSpec(x.shape, lambda i: (0,) * len(x.shape))
    return pl.pallas_call(
        final_kernel,
        grid=(1,),
        in_specs=[
            whole_of(sums),
            pl.BlockSpec((groups, SUB, lanes), lambda i: (0, rows // SUB - 1, 0)),
            whole_of(grads),
            whole_of(old),
            whole_of(param),
            whole_of(param),
            whole_of(param),
        ],
        out_specs=[whole_of(param), whole_of(param), whole_of(param), whole_of(old)],
        out_shape=[shape, shape, shape, jax.ShapeDtypeStruct(old.shape, jnp.float32)],
        compiler_params=params(),
    )(sums, every, grads, old, param, first_moment, second_moment)


def local(groups, blocks, hidden, latent_grad, lang_ids, old_weights, param, first_moment, second_moment):
    bits = blocks.bit_length() - 1
    rank = latent_grad.shape[2]

    def flip(even, odd):
        pairs = [(g * blocks + f, g * blocks + (f ^ (1 << (odd if g % 2 else even)))) for g in range(groups) for f in range(blocks)]
        return functools.partial(lax.ppermute, axis_name=BOTH, perm=pairs)

    hidden = pltpu.with_memory_space_constraint(hidden, pltpu.HBM)
    latent = pltpu.with_memory_space_constraint(latent_grad.transpose(0, 2, 1), pltpu.HBM)
    stage = [flip(k, 1 - k if k < 2 else k) for k in range(bits)]
    (send_far,) = slot_grads(hidden, latent, blocks, ((1, 1),), True)
    far = stage[0](send_far)
    (send_near,) = slot_grads(hidden, latent, blocks, ((0, 1),), True)
    near = stage[0](send_near)
    keep_far, keep_near = slot_grads(hidden, latent, blocks, ((1, 0), (0, 0)), False)
    for k in range(1, bits - 1):
        keep_far, send_far = middle(far, keep_far)
        far = stage[k](send_far)
        keep_near, send_near = middle(near, keep_near)
        near = stage[k](send_near)
    across = stage[bits - 1](passed(far, keep_far))
    mine = last(lang_ids[None], near, keep_near, across)
    every = lax.all_gather(mine, "language")
    sums = dots(every, rank)
    grads = turn(every)
    for k in range(bits):
        sums = sums + flip(k, k)(sums)
    new_param, new_first, new_second, logs = final(
        sums, every, grads, old_weights[None], param.T, first_moment.T, second_moment.T
    )
    return new_param.T, new_first.T, new_second.T, logs[0]


def solution(mesh):
    placed = (
        P("language", "fsdp", None),
        P("language", "fsdp", None),
        P("language"),
        P(),
        P("fsdp", None),
        P("fsdp", None),
        P("fsdp", None),
    )
    return jax.shard_map(
        functools.partial(local, mesh.shape["language"], mesh.shape["fsdp"]),
        mesh=mesh,
        in_specs=placed,
        out_specs=(P("fsdp", None), P("fsdp", None), P("fsdp", None), P()),
        check_vma=False,
    )
```

```python
import functools

import jax
import jax.numpy as jnp
from jax import lax
from jax.experimental import pallas as pl
from jax.experimental.pallas import tpu as pltpu
from jax.sharding import PartitionSpec as P


STEP = 100
SUB = 8
LANES = 128
FINE = 32.0
TOP = 32766.0
VMEM_LIMIT = 24 * 1024 * 1024
BOTH = ("language", "fsdp")


def whole(memory=pltpu.VMEM):
    return pl.BlockSpec(memory_space=memory)


def params():
    return pltpu.CompilerParams(vmem_limit_bytes=VMEM_LIMIT)


def encode(block):
    rows, lanes = block.shape
    half = rows // 2
    top = jnp.max(jnp.abs(block).reshape(rows // SUB, SUB, lanes), axis=0)
    step = jnp.ceil(jnp.log2(jnp.maximum(top, 1e-30)) * FINE)
    scale = jnp.exp2(step * (-1.0 / FINE)) * TOP
    codes = block.reshape(rows // SUB, SUB, lanes) * scale[None] + 32768.5
    codes = codes.astype(jnp.int32).reshape(rows, lanes)
    words = lax.shift_left(codes[:half], 16) | codes[half:]
    return words, step.astype(jnp.int32)


def decode(words, step):
    half, lanes = words.shape
    scale = jnp.exp2(step.astype(jnp.float32) * (1.0 / FINE)) * (1.0 / TOP)
    high = lax.shift_right_logical(words, 16).astype(jnp.float32) - 32768.0
    low = (words & 65535).astype(jnp.float32) - 32768.0
    both = jnp.concatenate([high, low], axis=0).reshape(2 * half // SUB, SUB, lanes)
    return (both * scale[None]).reshape(2 * half, lanes)


def place(blocks, parity, chain, half, index):
    bits = blocks.bit_length() - 1
    p = (half << parity) | (chain << (bits - 1))
    for k in range(1, bits - 1):
        bit = (index >> (bits - 2 - k)) & 1
        p |= bit << (1 - parity if k == 1 else k)
    return p


def grad_kernel(blocks, parts, coded, hidden_ref, latent_ref, *refs):
    out_refs, (hidden, latent, turned, sems) = refs[: len(parts)], refs[len(parts) :]
    count, slots, tokens, width = hidden.shape
    rank = latent.shape[1]
    rows = hidden_ref.shape[2] // blocks
    per = blocks // 4
    me, odd = lax.axis_index("fsdp"), lax.axis_index("language") % 2 == 1
    starts = []
    for chain, half in parts:
        for k in range(per):
            at_even, at_odd = place(blocks, 0, chain, half, k), place(blocks, 1, chain, half, k)
            starts.append(jnp.bitwise_xor(me, jnp.where(odd, at_odd, at_even)) * rows)
    small = pltpu.make_async_copy(latent_ref, latent, sems.at[count])
    small.start()
    copies, bases = [], []
    for k in range(count):
        base = jnp.minimum(starts[k] // LANES, (hidden_ref.shape[2] - width) // LANES) * LANES
        bases.append(pl.multiple_of(base, LANES))
        base = bases[k]
        copies.append(pltpu.make_async_copy(hidden_ref.at[:, :, pl.ds(base, width)], hidden.at[k], sems.at[k]))
        copies[k].start()
    small.wait()
    zero = jnp.zeros((rank, tokens), latent.dtype)
    left = jnp.concatenate(
        [jnp.concatenate([latent[a] if a == b else zero for b in range(slots)], axis=1) for a in range(slots)], axis=0
    )
    for k in range(count):
        copies[k].wait()
    for k in range(count):
        grad = jnp.dot(left, hidden[k].reshape(slots * tokens, width), preferred_element_type=jnp.float32)
        turned[k] = grad.T
    for k in range(count):
        block = turned[k, pl.ds(pl.multiple_of(starts[k] - bases[k], SUB), rows)]
        out_ref = out_refs[k // per]
        if coded:
            out_ref[k % per, : rows // 2], out_ref[k % per, rows // 2 :] = encode(block)
        else:
            out_ref[k % per] = block


def slot_grads(hidden, latent, blocks, parts, coded):
    slots, tokens, dim = hidden.shape
    rows = dim // blocks
    lanes = slots * latent.shape[1]
    reach = max(rows * k % LANES for k in range(blocks)) + rows
    width = pl.cdiv(reach, LANES) * LANES
    count = len(parts) * blocks // 4
    shape = (
        jax.ShapeDtypeStruct((blocks // 4, rows // 2 + SUB, lanes), jnp.int32)
        if coded
        else jax.ShapeDtypeStruct((blocks // 4, rows, lanes), jnp.float32)
    )
    return pl.pallas_call(
        functools.partial(grad_kernel, blocks, parts, coded),
        in_specs=[whole(pltpu.HBM), whole(pltpu.HBM)],
        out_specs=[whole()] * len(parts),
        out_shape=[shape] * len(parts),
        scratch_shapes=[
            pltpu.VMEM((count, slots, tokens, width), hidden.dtype),
            pltpu.VMEM(latent.shape, latent.dtype),
            pltpu.VMEM((count, width, lanes), jnp.float32),
            pltpu.SemaphoreType.DMA((count + 1,)),
        ],
        compiler_params=params(),
    )(hidden, latent)


def added(got_ref, keep_ref, at):
    half = got_ref.shape[1] - SUB
    return keep_ref[at] + decode(got_ref[at, :half], got_ref[at, half:])


def middle_kernel(got_ref, keep_ref, *refs):
    left_ref, send_ref = refs[-2:]
    blocks = keep_ref.shape[0]
    half = keep_ref.shape[1] // 2
    for k in range(blocks // 2):
        words, step = encode(added(got_ref, keep_ref, blocks // 2 + k))
        send_ref[k, :half] = words
        send_ref[k, half:] = step
    for k in range(blocks // 2):
        left_ref[k] = added(got_ref, keep_ref, k)


def middle(got, keep, *after):
    blocks, rows, lanes = keep.shape
    return pl.pallas_call(
        middle_kernel,
        in_specs=[whole(), whole()] + [whole(pl.ANY)] * len(after),
        out_specs=[whole(), whole()],
        out_shape=[
            jax.ShapeDtypeStruct((blocks // 2, rows, lanes), jnp.float32),
            jax.ShapeDtypeStruct((blocks // 2, rows // 2 + SUB, lanes), jnp.int32),
        ],
        compiler_params=params(),
    )(got, keep, *after)


def pass_kernel(got_ref, keep_ref, send_ref):
    half = keep_ref.shape[1] // 2
    send_ref[0, :half], send_ref[0, half:] = encode(added(got_ref, keep_ref, 0))


def passed(got, keep):
    return pl.pallas_call(
        pass_kernel,
        in_specs=[whole(), whole()],
        out_specs=whole(),
        out_shape=jax.ShapeDtypeStruct(got.shape, got.dtype),
        compiler_params=params(),
    )(got, keep)


def last_kernel(got_ref, keep_ref, across_ref, out_ref):
    half = keep_ref.shape[1] // 2
    out_ref[...] = added(got_ref, keep_ref, 0) + decode(across_ref[0, :half], across_ref[0, half:])


def last(got, keep, across):
    return pl.pallas_call(
        last_kernel,
        in_specs=[whole(), whole(), whole()],
        out_specs=whole(),
        out_shape=jax.ShapeDtypeStruct(keep.shape[1:], jnp.float32),
        compiler_params=params(),
    )(got, keep, across)


def spread(x, rank):
    lanes = x.shape[1]
    out = x
    shift = rank
    while shift < lanes:
        out = out + pltpu.roll(out, shift, 1)
        shift *= 2
    return out


def parity():
    return lax.axis_index("language") % 2


def positions(count):
    return (parity(), 1 - parity()) if count == 2 else tuple(range(count))


def dots_kernel(rank, *refs):
    grad_refs, out_ref = refs[:-1], refs[-1]
    groups = len(grad_refs)
    total = grad_refs[0][...]
    for ref in grad_refs[1:]:
        total = total + ref[...]
    total = spread(total, rank)
    row = lax.broadcasted_iota(jnp.int32, out_ref.shape, 0)
    out = jnp.where(row == groups, jnp.sum(total * total, axis=0, keepdims=True), 0.0)
    for at, ref in zip(positions(groups), grad_refs):
        out = jnp.where(row == at, jnp.sum(ref[...] * total, axis=0, keepdims=True), out)
    out_ref[...] = out


def dots(every, rank):
    return pl.pallas_call(
        functools.partial(dots_kernel, rank),
        in_specs=[whole()] * len(every),
        out_specs=whole(),
        out_shape=jax.ShapeDtypeStruct((pl.cdiv(len(every) + 1, SUB) * SUB, every[0].shape[1]), jnp.float32),
        compiler_params=params(),
    )(*every)


def turn_kernel(*refs):
    for at, ref in zip(positions(len(refs) - 1), refs):
        refs[-1][at] = ref[...].T


def turn(every):
    rows, lanes = every[0].shape
    return pl.pallas_call(
        turn_kernel,
        in_specs=[whole()] * len(every),
        out_specs=whole(),
        out_shape=jax.ShapeDtypeStruct((len(every), lanes, rows), jnp.float32),
        compiler_params=params(),
    )(*every)


def final_kernel(
    groups,
    sums_ref,
    got_ref,
    grad_ref,
    old_ref,
    param_ref,
    first_ref,
    second_ref,
    *refs,
):
    ids_refs, (new_param_ref, new_first_ref, new_second_ref, log_ref) = refs[:groups], refs[groups:]
    lanes = grad_ref.shape[1]
    langs = old_ref.shape[1]
    rank = param_ref.shape[0]
    slots = lanes // rank
    sums = sums_ref[...] + got_ref[...]
    parts = sums[:groups]
    square = jnp.sum(sums[groups : groups + 1, :rank], axis=1, keepdims=True) + 1e-06
    slot = lax.broadcasted_iota(jnp.int32, (groups, lanes), 1) // rank
    row = lax.broadcasted_iota(jnp.int32, (groups, lanes), 0)
    ids = jnp.zeros((groups, lanes), jnp.int32)
    for at, ref in zip(positions(groups), ids_refs):
        for k in range(slots):
            ids = jnp.where((slot == k) & (row == at), ref[:, k : k + 1], ids)
    at = lax.broadcasted_iota(jnp.int32, (1, langs), 1)
    align = jnp.zeros((1, langs), jnp.float32)
    for k in range(langs):
        one = jnp.sum(jnp.where(ids == k, parts, 0.0), axis=0, keepdims=True)
        align = jnp.where(at == k, jnp.sum(one, axis=1, keepdims=True), align)
    logits = jnp.log(old_ref[...]) + float(langs) * (align / square)
    logs = logits - jnp.log(jnp.sum(jnp.exp(logits), axis=1, keepdims=True))
    log_ref[...] = logs
    weights = jnp.exp(logs)
    update = None
    for g in range(groups):
        for s in range(slots):
            own = ids[g : g + 1, s * rank : s * rank + 1]
            weight = jnp.zeros((1, 1), jnp.float32)
            for k in range(langs):
                weight = weight + jnp.where(own == k, weights[:, k : k + 1], 0.0)
            term = weight * grad_ref[g, s * rank : (s + 1) * rank]
            update = term if update is None else update + term
    new_first = 0.9 * first_ref[...] + 0.1 * update
    new_second = 0.95 * second_ref[...] + 0.05 * update * update
    first_hat = new_first / (1.0 - 0.9**STEP)
    second_hat = new_second / (1.0 - 0.95**STEP)
    param = param_ref[...]
    new_param_ref[...] = param - 0.02 * (first_hat / (jnp.sqrt(second_hat) + 1e-08) + 0.1 * param)
    new_first_ref[...] = new_first
    new_second_ref[...] = new_second


def final(sums, got, grads, ids, old, param, first_moment, second_moment):
    shape = jax.ShapeDtypeStruct(param.shape, jnp.float32)
    return pl.pallas_call(
        functools.partial(final_kernel, len(ids)),
        in_specs=[whole()] * (7 + len(ids)),
        out_specs=[whole()] * 4,
        out_shape=[shape, shape, shape, jax.ShapeDtypeStruct(old.shape, jnp.float32)],
        compiler_params=params(),
    )(sums, got, grads, old, param, first_moment, second_moment, *ids)


def local(groups, blocks, hidden, latent_grad, lang_ids, old_weights, param, first_moment, second_moment):
    bits = blocks.bit_length() - 1
    rank = latent_grad.shape[2]

    def swap(x, even, odd, cross=0):
        pairs = []
        for g in range(groups):
            bit = odd if g % 2 else even
            pairs += [(g * blocks + f, (g ^ cross) * blocks + (f if bit is None else f ^ (1 << bit))) for f in range(blocks)]
        return lax.ppermute(x, BOTH, pairs)

    hidden = pltpu.with_memory_space_constraint(hidden, pltpu.HBM)
    latent = pltpu.with_memory_space_constraint(latent_grad.transpose(0, 2, 1), pltpu.HBM)
    far, near = 1, 0
    got, keep = {}, {}
    for c in (far, near):
        (out,) = slot_grads(hidden, latent, blocks, ((c, 1),), True)
        got[c] = swap(out, 0, 1)
    for c in (far, near):
        (keep[c],) = slot_grads(hidden, latent, blocks, ((c, 0),), False)
    ahead = []
    for k in range(1, bits):
        if k < bits - 1:
            keep[far], out = middle(got[far], keep[far])
        else:
            out = passed(got[far], keep[far])
        got[far] = swap(out, 1 if k == 1 else k, 0 if k == 1 else k)
        ahead.append(out)
    for k in range(1, bits - 1):
        keep[near], out = middle(got[near], keep[near], ahead[k])
        got[near] = swap(out, 1 if k == 1 else k, 0 if k == 1 else k)
    across = got[far]
    mine = last(got[near], keep[near], across)
    ids = lang_ids[None]
    if groups == 2:
        every = (mine, swap(mine, None, None, 1))
        ids = (ids, swap(ids, None, None, 1))
    else:
        every = tuple(lax.all_gather(mine, "language"))
        ids = tuple(lax.all_gather(ids, "language"))
    sums = dots(every, rank)
    grads = turn(every)
    for k in reversed(range(bits)):
        got = swap(sums, k, k, 1)
        if k > 0:
            sums = sums + got
    new_param, new_first, new_second, logs = final(
        sums, got, grads, ids, old_weights[None], param.T, first_moment.T, second_moment.T
    )
    return new_param.T, new_first.T, new_second.T, logs[0]


def solution(mesh):
    placed = (
        P("language", "fsdp", None),
        P("language", "fsdp", None),
        P("language"),
        P(),
        P("fsdp", None),
        P("fsdp", None),
        P("fsdp", None),
    )
    groups, blocks = mesh.shape["language"], mesh.shape["fsdp"]
    return jax.shard_map(
        functools.partial(local, groups, blocks),
        mesh=mesh,
        in_specs=placed,
        out_specs=(P("fsdp", None), P("fsdp", None), P("fsdp", None), P()),
        check_vma=False,
    )
```
